128 devices in a mesh: rows: 64 (over x_lo, y, z, core), feat: 2 (over x_hi).
Axes of the slice: x: 4 (x_hi: 2, x_lo: 2; x = x_hi * 2 + x_lo), y: 4, z: 4, core: 2. Of those that a mesh axis runs over, the one named last changes fastest.
Arguments:
- features: bfloat16 [65536, 256], P('rows', 'feat'), may hold values from -6 to 6
- weight: bfloat16 [256, 256], P('feat'), may hold values from -0.375 to 0.375
- cotangent: bfloat16 [65536, 256], P('rows', 'feat'), may hold values from -6 to 6
- tile_values: bfloat16 [6144, 128, 128], P('rows'), may hold values from -0.15625 to 0.15625
- tile_owner: int32 [6144, 1], P('rows'), may hold values from 0 to 63; in each aligned block of 96 rows (0 to 95, 96 to 191, ...) at most 2 rows name the same one
- tile_block: int32 [6144], P('rows'), may hold values from 0 to 7
- tile_dest: int32 [6144], P('rows'), may hold values from 0 to 7
- node_order: int32 [64, 1024], P('rows'), may hold values from 0 to 1023, each once within a row
Outputs:
- activated: bfloat16 [65536, 256], P('rows', 'feat')
- grad_features: bfloat16 [65536, 256], P('rows', 'feat')
- grad_weight: float32 [256, 256], P('feat')
The draws below stay inside these ranges and needn't reach their ends.
Inputs may be any that keep to these rules, and one draw needn't show every extreme that they name: `tile_owner`: among the 96 tiles of one device no owning device is named more than 2 times, and some owning device is named exactly 2 times. `node_order`: each row is a permutation of 0 to 1023.
All inputs are finite; a program needn't handle non-finite values.
Results may differ from the reference program's by a relative error of at most 0.0066.
Values may be sent and summed in bfloat16 or wider, within the bound.
A program may use at most 128 MiB of HBM per device.

```python
import math
import jax
import jax.numpy as jnp
import numpy as np
from jax import lax

TB = 128
BPD = 8
FEAT = 256
HID = 256
CAP = 2
TPD = 96
ROWS = 1024
NODES = 65536
NB = 512
TILES = 6144
N_ROWS = 64


def with_ends(values, rng, low, largest):
    place = [jax.random.randint(jax.random.fold_in(rng, axis), (), 0, length) for axis, length in enumerate(values.shape)]
    widest = values.shape.index(max(values.shape))
    next_to = place[:widest] + [(place[widest] + 1) % values.shape[widest]] + place[widest + 1:]
    return values.at[tuple(place)].set(low).at[tuple(next_to)].set(largest)


def shard_levels(own_key, dims, split, least, largest):
    factor_of = 1.0
    for position, shards_of in split:
        steps = jax.random.uniform(jax.random.fold_in(jax.random.fold_in(own_key, 6), position), (shards_of,), jnp.float32, least / len(split), largest / len(split))
        factor_of = factor_of * jnp.repeat(jnp.exp(steps), dims[position] // shards_of).reshape((-1,) + (1,) * (len(dims) - 1 - position))
    return factor_of


def deal_out(key, own, number, rows, number_of, top, bound, lean):
    sequence = jax.random.permutation(key, number_of)
    crowded, usual = shares(number_of, rows * top, bound, lean, True), shares(number_of, rows * top, bound, lean, False)
    places = jnp.arange(number_of)

    def named(tallies, turn):
        used = int((tallies > 0).sum())
        fixed = max(1, used // 4)
        passed = fixed + (places - fixed + turn * (used - fixed)) % max(1, number_of - fixed)
        return jnp.zeros((number_of,), jnp.int32).at[sequence[jnp.where(places < fixed, places, passed)]].set(jnp.asarray(tallies, jnp.int32))

    tallies = jnp.where(number % 4 == 0, named(crowded, number // 4), named(usual, number - number // 4 - 1))
    mixed = jax.random.permutation(jax.random.fold_in(own, 3), number_of)
    source_of, receiver = mixed[0:number_of // 2 * 2:2], mixed[1:number_of // 2 * 2:2]
    slack = jnp.minimum(tallies[source_of] - 1, bound - tallies[receiver]) // 2
    slack = jnp.where((source_of == sequence[0]) | (receiver == sequence[0]) | (tallies[receiver] == 0), 0, jnp.maximum(slack, 0))
    passed = jax.random.randint(jax.random.fold_in(own, 4), (number_of // 2,), 0, 1 << 20) % (slack + 1)
    tallies = tallies.at[source_of].add(-passed).at[receiver].add(passed)
    members = jnp.searchsorted(jnp.cumsum(tallies), jnp.arange(rows * top), side="right").astype(jnp.int32)
    table = members.reshape(top, rows).T
    table = table[jax.random.permutation(jax.random.fold_in(own, 1), rows)]
    turn = jax.random.randint(jax.random.fold_in(own, 2), (rows, 1), 0, top)
    return jnp.take_along_axis(table, (jnp.arange(top)[None, :] + turn) % top, axis=1)


def shares(count, total, limit, slope, full):
    weights = [(1 << 20) // math.isqrt(standing ** slope) + 1 for standing in range(1, count + 1)]
    largest = limit if full else min(limit, max(-(-total // count), total * weights[0] // sum(weights)))
    least = 1 if total - largest >= count - 1 else 0
    given, spare = [largest] + [least] * (count - 1), total - largest - least * (count - 1)
    while spare > 0:
        free = [i for i in range(1, count) if given[i] < largest] or [i for i in range(1, count) if given[i] < limit]
        mass, left = sum([weights[i] for i in free]), spare
        for i in free:
            addition = min(limit - given[i], max(1, left * weights[i] // mass), spare)
            given[i] = given[i] + addition
            spare = spare - addition
    return np.array(given)


def centred(rng, dims, width, bound, split=(), held_as=jnp.bfloat16):
    array = jax.random.normal(rng, dims, jnp.float32) * width
    if len(split) > 0:
        array = shard_levels(rng, dims, split, -0.22, 0.18) * array
    return jnp.clip(array, min=-bound, max=bound).astype(held_as)


def setup_inputs(seed: int = 0) -> dict:
    splits = jax.random.split(jax.random.key(seed), 9)
    features = centred(splits[0], (NODES, FEAT), 1.0, 6.0, ((0, 64), (1, 2)))
    weight = centred(splits[1], (FEAT, HID), FEAT ** -0.5, 0.375, ((0, 2),))
    cotangent = centred(splits[2], (NODES, HID), 1.0, 6.0, ((0, 64), (1, 2)))
    tile_values = centred(splits[3], (TILES, TB, TB), (TB * TPD // BPD) ** -0.5, 0.15625, ((0, 64),))
    tile_owner_keys = jax.random.split(jax.random.fold_in(splits[4], 1), TILES // TPD)
    tile_owner_turns = jax.random.permutation(jax.random.fold_in(splits[4], 3), TILES // TPD)
    tile_owner = jax.vmap(lambda own, number: deal_out(jax.random.fold_in(splits[4], 2), own, number, TPD, N_ROWS, 1, CAP, 2))(tile_owner_keys, tile_owner_turns).reshape((TILES, 1))
    tile_block = with_ends(jax.random.randint(splits[5], (TILES,), 0, BPD), jax.random.fold_in(splits[5], 1), 0, BPD - 1).astype(jnp.int32)
    tile_dest = with_ends(jax.random.randint(splits[6], (TILES,), 0, BPD), jax.random.fold_in(splits[6], 1), 0, BPD - 1).astype(jnp.int32)
    node_order = jax.vmap(lambda own: jax.random.permutation(own, ROWS))(jax.random.split(splits[7], N_ROWS)).reshape((N_ROWS, ROWS)).astype(jnp.int32)
    return {"features": features, "weight": weight, "cotangent": cotangent, "tile_values": tile_values, "tile_owner": tile_owner, "tile_block": tile_block, "tile_dest": tile_dest, "node_order": node_order}


def activation(inputs):
    return jax.nn.gelu(inputs, approximate=True)

def reference(features, weight, cotangent, tile_values, tile_owner, tile_block, tile_dest, node_order):
    global_rows = (jnp.arange(N_ROWS, dtype=jnp.int32)[:, None] * ROWS + node_order).reshape(-1).astype(jnp.int32)
    ordered = features[global_rows]
    cot_ordered = cotangent[global_rows]
    tile_stack = tile_values.reshape(N_ROWS, TPD, TB, TB)
    source_ids = (tile_owner[:, 0] * BPD + tile_block).reshape(N_ROWS, TPD).astype(jnp.int32)
    dest_local = tile_dest.reshape(N_ROWS, TPD).astype(jnp.int32)
    dest_ids = (dest_local + jnp.arange(N_ROWS, dtype=jnp.int32)[:, None] * BPD).astype(jnp.int32)
    feat_blocks = ordered.reshape(NB, TB, FEAT)

    def forward_dev(packed):
        tile_part, source_part, dest_part = packed
        blocks = feat_blocks[source_part].astype(jnp.float32)
        products = jnp.einsum('tij,tjc->tic', tile_part.astype(jnp.float32), blocks)
        return jax.ops.segment_sum(products, dest_part, num_segments=BPD)
    summed = lax.map(forward_dev, (tile_stack, source_ids, dest_local))
    aggregated = (ordered.astype(jnp.float32) + summed.reshape(NODES, FEAT)).astype(jnp.bfloat16)
    preact = jnp.dot(aggregated, weight, preferred_element_type=jnp.float32)
    act_values, pullback = jax.vjp(activation, preact)
    activated_rows = act_values.astype(jnp.bfloat16)
    grad_pre = pullback(cot_ordered.astype(jnp.float32))[0].astype(jnp.bfloat16)
    grad_weight = jnp.dot(aggregated.T, grad_pre, preferred_element_type=jnp.float32) * NODES ** (-0.5)
    grad_agg = jnp.dot(grad_pre, weight.T, preferred_element_type=jnp.float32).astype(jnp.bfloat16)
    grad_blocks = grad_agg.reshape(NB, TB, FEAT)

    def backward_dev(totals, packed):
        tile_part, source_part, dest_part = packed
        blocks = grad_blocks[dest_part].astype(jnp.float32)
        products = jnp.einsum('tji,tjc->tic', tile_part.astype(jnp.float32), blocks)
        return (totals.at[source_part].add(products), None)
    initial = jnp.zeros((NB, TB, FEAT), jnp.float32)
    totals, _ = lax.scan(backward_dev, initial, (tile_stack, source_ids, dest_ids))
    grad_rows = (grad_agg.astype(jnp.float32) + totals.reshape(NODES, FEAT)).astype(jnp.bfloat16)
    activated = jnp.zeros_like(activated_rows).at[global_rows].set(activated_rows)
    grad_features = jnp.zeros_like(grad_rows).at[global_rows].set(grad_rows)
    return (activated, grad_features, grad_weight)
```

```python
import jax
import jax.numpy as jnp
from jax import lax
from jax.experimental import pallas as pl
from jax.experimental.pallas import tpu as pltpu
import functools
from jax.sharding import PartitionSpec as P

CAP = 2
MESH = pl.DeviceIdType.MESH
NS = 120

def ag(G, ssem, rsem, x,y,z,c,f, fwd_partner=True):
    m4=lambda v: lax.rem(v+4,4)
    dev=lambda x_,y_,z_,c_: (((x_*4+y_)*4+z_)*2+c_, f)
    X=1-x
    A=lambda z_,y_,x_: (((c*4+z_)*4+y_)*2+x_)*3
    B=lambda y_,z_,x_: 192+(((c*4+y_)*4+z_)*2+x_)*3
    C1=lambda x_,z_,y_: 384+((c*2+x_)*4+z_)*4+y_
    C2=lambda x_,y_,z_: 448+((c*2+x_)*4+y_)*4+z_
    tgt={'x':dev(X,y,z,c),'y+':dev(x,m4(y+1),z,c),'y-':dev(x,m4(y-1),z,c),
         'z+':dev(x,y,m4(z+1),c),'z-':dev(x,y,m4(z-1),c),'c':dev(x,y,z,1-c)}
    names={}
    sent=[]
    def desc(name,ref_s,ref_d,to):
        i=names.setdefault(name,len(names))
        return pltpu.make_async_remote_copy(ref_s,ref_d,ssem.at[i],rsem.at[i],device_id=to,device_id_type=MESH)
    def view(idx,n,h=None):
        if h is None: return G.at[pl.ds(idx,n)]
        return G.at[idx,pl.ds(h*64,64)]
    def send(name,idx,n,to,h=None):
        v=view(idx,n,h)
        d=desc(name,v,v,tgt[to]); d.start(); sent.append(d)
    def fw(name,idx,n,h=None):
        if fwd_partner: send('p'+name,idx,n,'c',h); parts.append((name,n,h))
    parts=[]
    def wait(name,n,h=None):
        v=view(0,n,h)
        desc(name,v,v,tgt['c']).wait_recv()
    send('Cy+',C1(x,z,y),1,'y+'); send('Cy-',C1(x,z,y),1,'y-')
    send('Dz+',C2(x,y,z),1,'z+'); send('Dz-',C2(x,y,z),1,'z-')
    send('Ax',A(z,y,x),3,'x'); send('Bx',B(y,z,x),3,'x')
    send('Ay+o',A(z,y,x),3,'y+'); send('Ay-o',A(z,y,x),3,'y-')
    send('Bz+o',B(y,z,x),3,'z+'); send('Bz-o',B(y,z,x),3,'z-')
    fw('oA',A(z,y,x),3); fw('oB',B(y,z,x),3);
    yp,ym,y2=m4(y+1),m4(y-1),m4(y+2); zp,zm,z2=m4(z+1),m4(z-1),m4(z+2)
    wait('Ax',3); send('Ay+x',A(z,y,X),3,'y+'); send('Ay-x',A(z,y,X),3,'y-');
    wait('Bx',3); send('Bz+x',B(y,z,X),3,'z+'); send('Bz-x',B(y,z,X),3,'z-');
    wait('Cy+',1); send('Cy+f',C1(x,z,ym),1,'y+',0); wait('Cy-',1); send('Cy-f',C1(x,z,yp),1,'y-',1)
    wait('Dz+',1); send('Dz+f',C2(x,y,zm),1,'z+',0); wait('Dz-',1); send('Dz-f',C2(x,y,zp),1,'z-',1)
    send('Az+0',A(z,y,0),6,'z+'); send('Az-0',A(z,y,0),6,'z-')
    send('By+0',B(y,z,0),6,'y+'); send('By-0',B(y,z,0),6,'y-')
    fw('Ax',A(z,y,X),3); fw('Bx',B(y,z,X),3)
    wait('Ay+o',3); wait('Ay-o',3); wait('Ay+x',3); wait('Ay-x',3)
    send('Ay+f',A(z,ym,0),3,'y+'); send('Ay-f',A(z,yp,1),3,'y-')
    wait('Bz+o',3); wait('Bz-o',3); wait('Bz+x',3); wait('Bz-x',3)
    send('Bz+f',B(y,zm,0),3,'z+'); send('Bz-f',B(y,zp,1),3,'z-')
    wait('Cy+f',1,0); wait('Cy-f',1,1); send('Cz+',C1(x,z,0),4,'z+'); send('Cz-',C1(x,z,0),4,'z-')
    wait('Dz+f',1,0); wait('Dz-f',1,1); send('Dy+',C2(x,y,0),4,'y+'); send('Dy-',C2(x,y,0),4,'y-')
    send('Cx0',C1(x,z,0),4,'x'); send('Dx0',C2(x,y,0),4,'x')
    fw('C0',C1(x,z,0),4); fw('D0',C2(x,y,0),4)
    for k,yy in ((1,ym),(3,yp)):
        send(f'Az+{k}',A(z,yy,0),6,'z+'); send(f'Az-{k}',A(z,yy,0),6,'z-')
        fw(f'Ay{k}',A(z,yy,0),6)
    for k,zz in ((1,zm),(3,zp)):
        send(f'By+{k}',B(y,zz,0),6,'y+'); send(f'By-{k}',B(y,zz,0),6,'y-')
        fw(f'Bz{k}',B(y,zz,0),6)
    wait('Ay+f',3); wait('Ay-f',3)
    send('Az+2',A(z,y2,0),6,'z+'); send('Az-2',A(z,y2,0),6,'z-'); fw('Ay2',A(z,y2,0),6)
    wait('Bz+f',3); wait('Bz-f',3)
    send('By+2',B(y,z2,0),6,'y+'); send('By-2',B(y,z2,0),6,'y-'); fw('Bz2',B(y,z2,0),6)
    yk={0:y,1:ym,3:yp,2:y2}; zk={0:z,1:zm,3:zp,2:z2}
    def bulk(k):
        wait(f'Az+{k}',6); wait(f'Az-{k}',6)
        if k in (0,3): send(f'Az+f{k}',A(zm,yk[k],0),6,'z+')
        else: send(f'Az-f{k}',A(zp,yk[k],0),6,'z-')
        wait(f'By+{k}',6); wait(f'By-{k}',6)
        if k in (0,3): send(f'By+f{k}',B(ym,zk[k],0),6,'y+')
        else: send(f'By-f{k}',B(yp,zk[k],0),6,'y-')
        fw(f'Azm{k}',A(zm,yk[k],0),6); fw(f'Azp{k}',A(zp,yk[k],0),6)
        fw(f'Bym{k}',B(ym,zk[k],0),6); fw(f'Byp{k}',B(yp,zk[k],0),6)
    bulk(0)
    wait('Cz+',4); wait('Cz-',4); send('Cz+f',C1(x,zm,0),2,'z+'); send('Cz-f',C1(x,zp,2),2,'z-')
    wait('Dy+',4); wait('Dy-',4); send('Dy+f',C2(x,ym,0),2,'y+'); send('Dy-f',C2(x,yp,2),2,'y-')
    send('Cxm',C1(x,zm,0),4,'x'); send('Cxp',C1(x,zp,0),4,'x'); send('Dxm',C2(x,ym,0),4,'x'); send('Dxp',C2(x,yp,0),4,'x')
    fw('Czm',C1(x,zm,0),4); fw('Czp',C1(x,zp,0),4); fw('Dym',C2(x,ym,0),4); fw('Dyp',C2(x,yp,0),4)
    bulk(1)
    wait('Cz+f',2); wait('Cz-f',2); send('Cx2',C1(x,z2,0),4,'x'); fw('Cz2',C1(x,z2,0),4)
    wait('Dy+f',2); wait('Dy-f',2); send('Dx2',C2(x,y2,0),4,'x'); fw('Dy2',C2(x,y2,0),4)
    bulk(3);
    wait('Cx0',4); wait('Dx0',4); fw('Cx0',C1(X,z,0),4); fw('Dx0',C2(X,y,0),4)
    bulk(2)
    for s,zz,yy in (('m',zm,ym),('p',zp,yp),('2',z2,y2)):
        wait('Cx'+s,4); fw('Cx'+s,C1(X,zz,0),4); wait('Dx'+s,4); fw('Dx'+s,C2(X,yy,0),4)
    for k in (0,1,3,2):
        d='+' if k in (0,3) else '-'
        wait(f'Az{d}f{k}',6); fw(f'Az2{k}',A(z2,yk[k],0),6)
        wait(f'By{d}f{k}',6); fw(f'By2{k}',B(y2,zk[k],0),6)
    for name,n,h in parts: wait('p'+name,n,h)
    for d in sent: d.wait_send()

def kernel(fwdp, xin, o, G, ssem, rsem, lsem):
    me=lax.axis_index("rows"); f=lax.axis_index("feat")
    x=me//32; y=lax.rem(me//8,4); z=lax.rem(me//2,4); c=lax.rem(me,2)
    m4=lambda v: lax.rem(v+4,4)
    dev=lambda x_,y_,z_,c_: (((x_*4+y_)*4+z_)*2+c_, f)
    bar=pltpu.get_barrier_semaphore()
    for d in (dev(1-x,y,z,c),dev(x,m4(y+1),z,c),dev(x,m4(y-1),z,c),dev(x,y,m4(z+1),c),dev(x,y,m4(z-1),c),dev(x,y,z,1-c)):
        pl.semaphore_signal(bar,1,device_id=d,device_id_type=MESH)
    a=(((c*4+z)*4+y)*2+x)*3; b=192+(((c*4+y)*4+z)*2+x)*3; c1=384+((c*2+x)*4+z)*4+y; c2=448+((c*2+x)*4+y)*4+z
    cps=[pltpu.make_async_copy(xin.at[pl.ds(0,3)],G.at[pl.ds(a,3)],lsem.at[0]),
         pltpu.make_async_copy(xin.at[pl.ds(3,3)],G.at[pl.ds(b,3)],lsem.at[1]),
         pltpu.make_async_copy(xin.at[pl.ds(6,1)],G.at[pl.ds(c1,1)],lsem.at[2]),
         pltpu.make_async_copy(xin.at[pl.ds(7,1)],G.at[pl.ds(c2,1)],lsem.at[3])]
    for q in cps: q.start()
    for q in cps: q.wait()
    pl.semaphore_wait(bar,6)
    ag(G,ssem,rsem,x,y,z,c,f,fwdp)
    q=pltpu.make_async_copy(G,o,lsem.at[0])
    q.start()
    q.wait()


def activation(inputs):
    return jax.nn.gelu(inputs, approximate=True)


def local(features, weight, cotangent, tile_values, tile_owner, tile_block, tile_dest, node_order):
    rows_here = features.shape[0]
    feat_width = features.shape[1]
    tile_size = tile_values.shape[1]
    tile_count = tile_values.shape[0]
    peer_count = lax.axis_size("rows")
    blocks_here = rows_here // tile_size
    local_order = node_order[0]
    ordered = features[local_order]
    cot_ordered = cotangent[local_order]
    owners = tile_owner[:, 0]
    owner_hits = (owners[:, None] == jnp.arange(peer_count, dtype=jnp.int32)[None, :]).astype(
        jnp.int32
    )
    slot_rank = jnp.sum((jnp.cumsum(owner_hits, axis=0) - owner_hits) * owner_hits, axis=1)
    flat_slot = owners * CAP + slot_rank
    slot_blocks = (
        jnp.full((peer_count * CAP,), blocks_here, jnp.int32).at[flat_slot].set(tile_block)
    )
    slot_blocks = slot_blocks.reshape(peer_count, CAP)
    dest_hot = (jnp.arange(blocks_here, dtype=jnp.int32)[:, None] == tile_dest[None, :]).astype(
        jnp.float32
    )
    gathered = pl.pallas_call(
        functools.partial(kernel, True),
        out_shape=jax.ShapeDtypeStruct((512, 128, 128), jnp.bfloat16),
        in_specs=[pl.BlockSpec(memory_space=pl.ANY)],
        out_specs=pl.BlockSpec(memory_space=pl.ANY),
        scratch_shapes=[pltpu.VMEM((512,128,128),jnp.bfloat16),pltpu.SemaphoreType.DMA((NS,)),pltpu.SemaphoreType.DMA((NS,)),pltpu.SemaphoreType.DMA((4,))],
        compiler_params=pltpu.CompilerParams(collective_id=0,has_side_effects=True,vmem_limit_bytes=60<<20),
    )(ordered.reshape(8, 128, 128))
    ox, oy, oz, oc = owners // 32, owners // 8 % 4, owners // 2 % 4, owners % 2
    fA = (((oc * 4 + oz) * 4 + oy) * 2 + ox) * 3 + tile_block
    fB = 192 + (((oc * 4 + oy) * 4 + oz) * 2 + ox) * 3 + tile_block - 3
    fC = 384 + ((oc * 2 + ox) * 4 + oz) * 4 + oy
    fD = 448 + ((oc * 2 + ox) * 4 + oy) * 4 + oz
    flat = jnp.where(tile_block < 3, fA, jnp.where(tile_block < 6, fB, jnp.where(tile_block == 6, fC, fD)))
    sources = gathered[flat]
    fwd_products = jnp.einsum(
        "tij,tjc->tic", tile_values, sources, preferred_element_type=jnp.float32
    )
    summed = jnp.dot(
        dest_hot, fwd_products.reshape(tile_count, -1), precision=lax.Precision.HIGHEST
    )
    aggregated = (ordered.astype(jnp.float32) + summed.reshape(rows_here, feat_width)).astype(
        jnp.bfloat16
    )
    partial_pre = jnp.dot(aggregated, weight, preferred_element_type=jnp.float32)
    preact = lax.psum_scatter(partial_pre, "feat", scatter_dimension=1, tiled=True)
    act_values, pullback = jax.vjp(activation, preact)
    activated_rows = act_values.astype(jnp.bfloat16)
    grad_pre = pullback(cot_ordered.astype(jnp.float32))[0].astype(jnp.bfloat16)
    grad_full = lax.all_gather(grad_pre, "feat", axis=1, tiled=True)
    node_count = rows_here * peer_count
    weight_part = jnp.einsum("rf,rh->fh", aggregated, grad_full, preferred_element_type=jnp.float32)
    grad_weight = lax.psum(weight_part, "rows") * node_count ** (-0.5)
    grad_agg = jnp.einsum(
        "rh,fh->rf", grad_full, weight, preferred_element_type=jnp.float32
    ).astype(jnp.bfloat16)
    dest_rows = grad_agg.reshape(blocks_here, tile_size, feat_width)[tile_dest]
    back_products = jnp.einsum(
        "tji,tjc->tic", tile_values, dest_rows, preferred_element_type=jnp.float32
    )
    outgoing = (
        jnp.zeros((peer_count * CAP, tile_size, feat_width), jnp.bfloat16)
        .at[flat_slot]
        .set(back_products.astype(jnp.bfloat16))
    )
    outgoing = outgoing.reshape(peer_count, CAP, tile_size, feat_width)
    incoming, owner_blocks = (
        lax.all_to_all(outgoing, "rows", split_axis=0, concat_axis=0, tiled=True),
        lax.all_to_all(slot_blocks, "rows", split_axis=0, concat_axis=0, tiled=True),
    )
    owner_hot = (
        jnp.arange(blocks_here, dtype=jnp.int32)[:, None] == owner_blocks.reshape(1, -1)
    ).astype(jnp.float32)
    adjoint_sum = jnp.dot(
        owner_hot.astype(jnp.bfloat16), incoming.reshape(peer_count * CAP, -1), preferred_element_type=jnp.float32
    )
    grad_rows = (grad_agg.astype(jnp.float32) + adjoint_sum.reshape(rows_here, feat_width)).astype(
        jnp.bfloat16
    )
    inverse = (
        jnp.zeros_like(local_order).at[local_order].set(jnp.arange(rows_here, dtype=jnp.int32))
    )
    return (activated_rows[inverse], grad_rows[inverse], grad_weight)


def solution(mesh):
    return jax.shard_map(
        local,
        mesh=mesh,
        in_specs=(
            P("rows", "feat"),
            P("feat", None),
            P("rows", "feat"),
            P("rows", None, None),
            P("rows", None),
            P("rows"),
            P("rows"),
            P("rows", None),
        ),
        out_specs=(P("rows", "feat"), P("rows", "feat"), P("feat", None)),
        check_vma=False,
    )
```

```python
import jax
import jax.numpy as jnp
from jax import lax
from jax.experimental import pallas as pl
from jax.experimental.pallas import tpu as pltpu
from jax.sharding import PartitionSpec as P

MESH = pl.DeviceIdType.MESH
F32, BF16, I32 = jnp.float32, jnp.bfloat16, jnp.int32
NS = 190
F_TILE, F_SRC, F_DEST, F_CUM, B_TILE, B_DEST, B_BLK = range(7)


class Net:
    def __init__(self, ssem, rsem, targets):
        self.ssem, self.rsem, self.targets = ssem, rsem, targets
        self.names, self.sent = {}, []

    def copy(self, name, src, dst, to):
        i = self.names.setdefault(name, len(self.names))
        return pltpu.make_async_remote_copy(
            src, dst, self.ssem.at[i], self.rsem.at[i], device_id=self.targets[to], device_id_type=MESH
        )

    def send(self, name, src, dst, to):
        d = self.copy(name, src, dst, to)
        d.start()
        self.sent.append(d)

    def wait(self, name, view):
        self.copy(name, view, view, "c").wait_recv()

    def drain(self):
        for d in self.sent:
            d.wait_send()


def gather_blocks(G, net, x, y, z, c, fill):
    m4 = lambda v: lax.rem(v + 4, 4)
    X = 1 - x
    A = lambda z_, y_, x_: (((c * 4 + z_) * 4 + y_) * 2 + x_) * 3
    B = lambda y_, z_, x_: 192 + (((c * 4 + y_) * 4 + z_) * 2 + x_) * 3
    C1 = lambda x_, z_, y_: 384 + ((c * 2 + x_) * 4 + z_) * 4 + y_
    C2 = lambda x_, y_, z_: 448 + ((c * 2 + x_) * 4 + y_) * 4 + z_
    parts = []

    def view(idx, n, h=None):
        if h is None:
            return G.at[pl.ds(idx, n)]
        return G.at[idx, pl.ds(h * 64, 64)]

    def send(name, idx, n, to, h=None):
        v = view(idx, n, h)
        net.send(name, v, v, to)

    def fw(name, idx, n, h=None):
        send("p" + name, idx, n, "c", h)
        parts.append((name, n, h))

    def wait(name, n, h=None):
        net.wait(name, view(0, n, h))

    send('Cy+',C1(x,z,y),1,'y+'); send('Cy-',C1(x,z,y),1,'y-')
    send('Dz+',C2(x,y,z),1,'z+'); send('Dz-',C2(x,y,z),1,'z-')
    send('Ax',A(z,y,x),3,'x'); send('Bx',B(y,z,x),3,'x')
    send('Ay+o',A(z,y,x),3,'y+'); send('Ay-o',A(z,y,x),3,'y-')
    send('Bz+o',B(y,z,x),3,'z+'); send('Bz-o',B(y,z,x),3,'z-')
    fw('oA',A(z,y,x),3); fw('oB',B(y,z,x),3);
    yp,ym,y2=m4(y+1),m4(y-1),m4(y+2); zp,zm,z2=m4(z+1),m4(z-1),m4(z+2)
    wait('Ax',3); send('Ay+x',A(z,y,X),3,'y+'); send('Ay-x',A(z,y,X),3,'y-');
    wait('Bx',3); send('Bz+x',B(y,z,X),3,'z+'); send('Bz-x',B(y,z,X),3,'z-');
    wait('Cy+',1); send('Cy+f',C1(x,z,ym),1,'y+',0); wait('Cy-',1); send('Cy-f',C1(x,z,yp),1,'y-',1)
    wait('Dz+',1); send('Dz+f',C2(x,y,zm),1,'z+',0); wait('Dz-',1); send('Dz-f',C2(x,y,zp),1,'z-',1)
    send('Az+0',A(z,y,0),6,'z+'); send('Az-0',A(z,y,0),6,'z-')
    send('By+0',B(y,z,0),6,'y+'); send('By-0',B(y,z,0),6,'y-')
    fw('Ax',A(z,y,X),3); fw('Bx',B(y,z,X),3)
    wait('Ay+o',3); wait('Ay-o',3); wait('Ay+x',3); wait('Ay-x',3)
    send('Ay+f',A(z,ym,0),3,'y+'); send('Ay-f',A(z,yp,1),3,'y-')
    wait('Bz+o',3); wait('Bz-o',3); wait('Bz+x',3); wait('Bz-x',3)
    send('Bz+f',B(y,zm,0),3,'z+'); send('Bz-f',B(y,zp,1),3,'z-')
    wait('Cy+f',1,0); wait('Cy-f',1,1); send('Cz+',C1(x,z,0),4,'z+'); send('Cz-',C1(x,z,0),4,'z-')
    wait('Dz+f',1,0); wait('Dz-f',1,1); send('Dy+',C2(x,y,0),4,'y+'); send('Dy-',C2(x,y,0),4,'y-')
    send('Cx0',C1(x,z,0),4,'x'); send('Dx0',C2(x,y,0),4,'x')
    fw('C0',C1(x,z,0),4); fw('D0',C2(x,y,0),4)
    fill()
    for k,yy in ((1,ym),(3,yp)):
        send(f'Az+{k}',A(z,yy,0),6,'z+'); send(f'Az-{k}',A(z,yy,0),6,'z-')
        fw(f'Ay{k}',A(z,yy,0),6)
    for k,zz in ((1,zm),(3,zp)):
        send(f'By+{k}',B(y,zz,0),6,'y+'); send(f'By-{k}',B(y,zz,0),6,'y-')
        fw(f'Bz{k}',B(y,zz,0),6)
    fill()
    wait('Ay+f',3); wait('Ay-f',3)
    send('Az+2',A(z,y2,0),6,'z+'); send('Az-2',A(z,y2,0),6,'z-'); fw('Ay2',A(z,y2,0),6)
    wait('Bz+f',3); wait('Bz-f',3)
    send('By+2',B(y,z2,0),6,'y+'); send('By-2',B(y,z2,0),6,'y-'); fw('Bz2',B(y,z2,0),6)
    yk={0:y,1:ym,3:yp,2:y2}; zk={0:z,1:zm,3:zp,2:z2}
    def bulk(k):
        wait(f'Az+{k}',6); wait(f'Az-{k}',6)
        if k in (0,3): send(f'Az+f{k}',A(zm,yk[k],0),6,'z+')
        else: send(f'Az-f{k}',A(zp,yk[k],0),6,'z-')
        wait(f'By+{k}',6); wait(f'By-{k}',6)
        if k in (0,3): send(f'By+f{k}',B(ym,zk[k],0),6,'y+')
        else: send(f'By-f{k}',B(yp,zk[k],0),6,'y-')
        fw(f'Azm{k}',A(zm,yk[k],0),6); fw(f'Azp{k}',A(zp,yk[k],0),6)
        fw(f'Bym{k}',B(ym,zk[k],0),6); fw(f'Byp{k}',B(yp,zk[k],0),6)
    fill()
    bulk(0)
    fill()
    wait('Cz+',4); wait('Cz-',4); send('Cz+f',C1(x,zm,0),2,'z+'); send('Cz-f',C1(x,zp,2),2,'z-')
    wait('Dy+',4); wait('Dy-',4); send('Dy+f',C2(x,ym,0),2,'y+'); send('Dy-f',C2(x,yp,2),2,'y-')
    send('Cxm',C1(x,zm,0),4,'x'); send('Cxp',C1(x,zp,0),4,'x'); send('Dxm',C2(x,ym,0),4,'x'); send('Dxp',C2(x,yp,0),4,'x')
    fw('Czm',C1(x,zm,0),4); fw('Czp',C1(x,zp,0),4); fw('Dym',C2(x,ym,0),4); fw('Dyp',C2(x,yp,0),4)
    fill()
    bulk(1)
    fill()
    wait('Cz+f',2); wait('Cz-f',2); send('Cx2',C1(x,z2,0),4,'x'); fw('Cz2',C1(x,z2,0),4)
    wait('Dy+f',2); wait('Dy-f',2); send('Dx2',C2(x,y2,0),4,'x'); fw('Dy2',C2(x,y2,0),4)
    fill()
    bulk(3)
    fill()
    wait('Cx0',4); wait('Dx0',4); fw('Cx0',C1(X,z,0),4); fw('Dx0',C2(X,y,0),4)
    bulk(2)
    fill()
    for s,zz,yy in (('m',zm,ym),('p',zp,yp),('2',z2,y2)):
        wait('Cx'+s,4); fw('Cx'+s,C1(X,zz,0),4); wait('Dx'+s,4); fw('Dx'+s,C2(X,yy,0),4)
    for k in (0,1,3,2):
        d='+' if k in (0,3) else '-'
        wait(f'Az{d}f{k}',6); fw(f'Az2{k}',A(z2,yk[k],0),6)
        wait(f'By{d}f{k}',6); fw(f'By2{k}',B(y2,zk[k],0),6)
    fill()
    for name,n,h in parts: wait('p'+name,n,h)


def dot(a, b):
    return jnp.dot(a, b, preferred_element_type=F32)


def loop(n, body, unroll):
    def step(i, carry):
        body(i)
        return carry

    lax.fori_loop(0, n, step, 0, unroll=unroll)


def index_tables(pack, TAB):
    owner, block, dest = pack[0:1, :], pack[1:2, :], pack[2:3, :]
    sq = (128, 128)
    row = lambda v: jnp.broadcast_to(v, sq)
    col = lambda v: jnp.broadcast_to(v, sq).T
    i, j = lax.broadcasted_iota(I32, sq, 0), lax.broadcasted_iota(I32, sq, 1)
    count = lambda m: jnp.sum(jnp.where(m, 1, 0), axis=0, keepdims=True)
    co, cd, cb = col(owner), col(dest), col(block)
    rank = count((co == row(owner)) & (i < j))
    place = count((cd < row(dest)) | ((cd == row(dest)) & (i < j)))
    ox, oy, oz, oc = owner >> 5, (owner >> 3) & 3, (owner >> 1) & 3, owner & 1
    fa = (((oc * 4 + oz) * 4 + oy) * 2 + ox) * 3 + block
    fb = 192 + (((oc * 4 + oy) * 4 + oz) * 2 + ox) * 3 + block - 3
    fc = 384 + ((oc * 2 + ox) * 4 + oz) * 4 + oy
    fd = 448 + ((oc * 2 + ox) * 4 + oy) * 4 + oz
    src = jnp.where(block < 3, fa, jnp.where(block < 6, fb, jnp.where(block == 6, fc, fd)))
    op, os = jnp.where(oc == 0, oz, oy), jnp.where(oc == 0, oy, oz)
    slot = (((oc * 4 + op) * 2 + ox) * 4 + os) * 2 + rank
    live = lax.broadcasted_iota(I32, (1, 128), 1) < 96
    slot = jnp.where(live, slot, 999)
    cp, cs = col(place), col(slot)
    pick = lambda m, v: jnp.sum(jnp.where(m, v, 0), axis=0, keepdims=True)
    at_place, at_slot = cp == j, cs == j
    rows = [
        pick(at_place, i),
        pick(at_place, col(src)),
        pick(at_place, cd),
        count((cd <= j) & (i < 96)),
        pick(at_slot, i),
        pick(at_slot, cd),
        pick(at_slot, cb + 1) - 1,
    ]
    for r, (v, most) in enumerate(zip(rows, (95, 511, 7, 96, 95, 7, 7))):
        TAB[r : r + 1, :] = jnp.clip(v, -1 if r == B_BLK else 0, most)


def kernel(
    pack, order, feat, wt, cot, tiles, act_o, gf_o, gw_o,
    G, T, ST, SEG, PM, QM, CO, WO, WR, WOR, COT, AGG, AGO, GP, GA, OS, PP, RP, RL, D, RD, RL2, FX, FR, ACT,
    TAB, TABS, TV, TVS, WG, WZ, W2, WS, W3, WX, W4, WC, WF, ssem, rsem, lsem,
):
    me, f = lax.axis_index("rows"), lax.axis_index("feat")
    x, y, z, c = me // 32, lax.rem(me // 8, 4), lax.rem(me // 2, 4), lax.rem(me, 2)
    p, s = (1 - c) * z + c * y, (1 - c) * y + c * z
    X, e = 1 - x, 1 - c
    m4 = lambda v: lax.rem(v + 4, 4)
    dev = lambda x_, y_, z_, c_: (((x_ * 4 + y_) * 4 + z_) * 2 + c_, f)
    dps = lambda p_, s_, c_: dev(x, (1 - c) * s_ + c * p_, (1 - c) * p_ + c * s_, c_)
    targets = {
        "x": dev(X, y, z, c), "y+": dev(x, m4(y + 1), z, c), "y-": dev(x, m4(y - 1), z, c),
        "z+": dev(x, y, m4(z + 1), c), "z-": dev(x, y, m4(z - 1), c), "c": dev(x, y, z, e), "f": (me, 1 - f),
    }
    for k in (1, 2, 3):
        targets[f"p{k}"], targets[f"s{k}"] = dps(m4(p + k), s, c), dps(p, m4(s + k), c)
        targets[f"P{k}"], targets[f"S{k}"] = dps(m4(p + k), s, e), dps(p, m4(s + k), e)
        targets[f"z{k}"], targets[f"y{k}"] = dev(x, y, m4(z + k), c), dev(x, m4(y + k), z, c)
    entry = lambda r, i, most: jnp.clip(TABS[r, i], 0, most)
    peers = ["x", "f", "c"] + [a + str(k) for a in "psPS" for k in (1, 2, 3)]
    bar = pltpu.get_barrier_semaphore()
    for n in peers:
        pl.semaphore_signal(bar, 1, device_id=targets[n], device_id_type=MESH)
    net = Net(ssem, rsem, targets)
    tile_copy = pltpu.make_async_copy(tiles, T, lsem.at[0])
    tile_copy.start()

    a0, b0 = (((c * 4 + z) * 4 + y) * 2 + x) * 3, 192 + (((c * 4 + y) * 4 + z) * 2 + x) * 3
    c0, d0 = 384 + ((c * 2 + x) * 4 + z) * 4 + y, 448 + ((c * 2 + x) * 4 + y) * 4 + z
    place = [a0, a0 + 1, a0 + 2, b0, b0 + 1, b0 + 2, c0, d0]
    lanes = lax.broadcasted_iota(I32, (128, 1024), 1).astype(F32)
    order_f = order[...].astype(F32)
    for b in range(8):
        oc = jnp.broadcast_to(order_f[:, b * 128 : (b + 1) * 128], (128, 128)).T
        hot = jnp.where(jnp.concatenate([oc] * 8, axis=1) == lanes, 1.0, 0.0).astype(BF16)
        PM[b] = hot
        G[place[b]] = dot(hot, feat[...]).astype(BF16)
    pl.semaphore_wait(bar, len(peers))

    def early():
        net.send("cot", cot, CO, "f")
        net.send("wt", wt, WO, "f")
        index_tables(pack, TAB)
        TV[p * 2 + c] = jnp.broadcast_to(TAB[B_BLK : B_BLK + 1, :], (8, 128))
        q = pltpu.make_async_copy(TAB, TABS, lsem.at[1])
        q.start()
        for k in (1, 2, 3):
            net.send(f"t{k}", TV.at[p * 2 + c], TV.at[p * 2 + c], f"p{k}")
        for k in (0, 1, 2, 3):
            net.send(f"u{k}", TV.at[p * 2 + c], TV.at[s * 2 + c], f"S{k}" if k else "c")
        q.wait()
        tile_copy.wait()

    def transposed(lo):
        def body(i):
            ST[lo + i] = T[entry(B_TILE, lo + i, 95)].T

        return lambda: loop(32, body, 8)

    def weights():
        net.wait("wt", WO)
        for src, dst in ((wt, WR), (WO, WOR)):
            v = src[...]
            u = jnp.concatenate([v[:, 128:], v[:, :128]], axis=1)
            dst[...] = jnp.where(f == 0, v, u)
        net.wait("cot", CO)

    def cotangents():
        def body(b):
            COT[b, :, 0:128] = dot(PM[b], cot[...]).astype(BF16)
            COT[b, :, 128:256] = dot(PM[b], CO[...]).astype(BF16)

        loop(8, body, 1)

    def inverse():
        def body(b):
            j = (lax.broadcasted_iota(I32, (128, 1024), 0) + b * 128).astype(F32)
            QM[b] = jnp.where(jnp.broadcast_to(order_f, (128, 1024)) == j, 1.0, 0.0).astype(BF16)

        loop(8, body, 1)

    def block_tables():
        for k in (1, 2, 3):
            net.wait(f"t{k}", TV.at[0])
        for k in (0, 1, 2, 3):
            net.wait(f"u{k}", TV.at[0])
        q = pltpu.make_async_copy(TV, TVS, lsem.at[1])
        q.start()
        q.wait()

    fillers = [early, transposed(0), transposed(32), transposed(64), transposed(96), weights, cotangents, inverse, block_tables]

    def fill():
        if fillers:
            fillers.pop(0)()

    gather_blocks(G, net, x, y, z, c, fill)
    while fillers:
        fill()

    def product(i, total):
        fresh = (i == 0) | (TABS[F_DEST, i] != TABS[F_DEST, jnp.maximum(i - 1, 0)])
        total = total * jnp.where(fresh, 0.0, 1.0) + dot(T[entry(F_TILE, i, 95)], G[entry(F_SRC, i, 511)])
        SEG[i] = total
        return total

    lax.fori_loop(0, 96, product, jnp.zeros((128, 128), F32), unroll=8)
    for b in range(8):
        last = TABS[F_CUM, b]
        first = TABS[F_CUM, b - 1] if b else 0
        some = jnp.where(last > first, 1.0, 0.0)
        AGG[b] = (G[place[b]].astype(F32) + SEG[jnp.clip(last - 1, 0, 95)] * some).astype(BF16)
        net.send(f"agg{b}", AGG.at[b], AGO.at[b], "f")

    for b in range(8):
        net.wait(f"agg{b}", AGO.at[b])
        own = AGG[b]
        v = dot(own, WR[...]) + dot(AGO[b], WOR[...])
        t = jnp.tanh(0.7978845608 * (v + 0.044715 * (v * v * v)))
        half = 0.5 * (1.0 + t)
        ACT[b] = (v[:, :128] * half[:, :128]).astype(BF16)
        slope = half + 0.5 * v * (1.0 - t * t) * (0.7978845608 * (1.0 + 0.134145 * (v * v)))
        gp = (COT[b].astype(F32) * slope).astype(BF16)
        GA[b] = lax.dot_general(gp, WR[...], (((1,), (1,)), ((), ())), preferred_element_type=F32).astype(BF16)
        part = dot(own.T, gp)
        for q in range(4):
            rows = part[q * 32 : (q + 1) * 32]
            WG[q] = rows if b == 0 else WG[q] + rows

    for k in (1, 2, 3):
        net.send(f"wp{k}", WG.at[m4(z + k)], WZ.at[z], f"z{k}")

    def weight_1():
        for k in (1, 2, 3):
            net.wait(f"wp{k}", WZ.at[0])
        total = WG[z] + WZ[m4(z + 1)] + WZ[m4(z + 2)] + WZ[m4(z + 3)]
        for q in range(4):
            W2[q] = total[q * 8 : (q + 1) * 8]
        for k in (1, 2, 3):
            net.send(f"ws{k}", W2.at[m4(y + k)], WS.at[y], f"y{k}")

    def weight_2():
        for k in (1, 2, 3):
            net.wait(f"ws{k}", WS.at[0])
        W3[...] = W2[y] + WS[m4(y + 1)] + WS[m4(y + 2)] + WS[m4(y + 3)]
        net.send("wx", W3, WX, "x")

    def weight_3():
        net.wait("wx", WX)
        W4[...] = W3[...] + WX[...]
        net.send("wc", W4, WC, "c")

    def weight_4():
        net.wait("wc", WC)
        WF[z, y] = W4[...] + WC[...]
        for k in (1, 2, 3):
            net.send(f"wt{k}", WF.at[z, y], WF.at[z, y], f"y{k}")

    def weight_5():
        for k in (1, 2, 3):
            net.wait(f"wt{k}", WF.at[0, 0])
        for k in (1, 2, 3):
            net.send(f"wq{k}", WF.at[z], WF.at[z], f"z{k}")

    pp, ps = s, p

    def products(plane, p_, h, out):
        base = ((plane * 4 + p_) * 2 + h) * 8

        def body(i):
            out[i // 2, lax.rem(i, 2)] = dot(ST[base + i], GA[entry(B_DEST, base + i, 7)]).astype(BF16)

        loop(8, body, 8)

    def slab(h, k, own):
        q = m4(p + k)
        return (RP if k == 0 else PP).at[q, h]

    for tag, h in (("X", X), ("x", x)):
        for k in (2, 1, 3, 0):
            q, mine = m4(pp + k), m4(p + k)
            products(e, q, h, OS.at[q, h])
            net.send(f"i{tag}{k}", OS.at[q, h], (RP if k == 0 else PP).at[q, h, c], "c")
            products(c, mine, h, slab(h, k, True).at[c])
        for k in (2, 1, 3, 0):
            v = slab(h, k, True)
            net.wait(f"i{tag}{k}", v.at[0])
            if k == 2:
                net.send(f"r+{tag}", v.at[0], RL.at[0, h], "p1")
                net.send(f"r-{tag}", v.at[1], RL.at[1, h], "p3")
            elif k:
                net.send(f"d{k}{tag}", v, RP.at[p, h], f"p{k}")

    def forward_p(tag, h):
        net.wait(f"r+{tag}", RL.at[0, 0])
        net.send(f"g+{tag}", RL.at[0, h], RP.at[m4(p - 1), h, 0], "p1")
        net.wait(f"r-{tag}", RL.at[0, 0])
        net.send(f"g-{tag}", RL.at[1, h], RP.at[m4(p + 1), h, 1], "p3")

    def wait_p(tag):
        for k in (1, 3):
            net.wait(f"d{k}{tag}", RP.at[0, 0])
        net.wait(f"g+{tag}", RP.at[0, 0, 0])
        net.wait(f"g-{tag}", RP.at[0, 0, 0])

    def combine(tag, h):
        def owner(s_):
            q = (((c * 4 + p) * 2 + h) * 4 + s_) * 2
            marks = [[TVS[n, 0, q + r] for r in (0, 1)] for n in range(8)]
            weights_ = [
                [[jnp.where(marks[n][r] == b, 1.0, 0.0) for b in range(8)] for r in (0, 1)] for n in range(8)
            ]

            def chunk(i, carry):
                at = pl.ds(i * 16, 16)
                sums = [jnp.zeros((16, 128), F32) for _ in range(8)]
                for n in range(8):
                    for r in (0, 1):
                        v = RP[n // 2, h, n % 2, s_, r, at, :].astype(F32)
                        sums = [t + v * weights_[n][r][b] for b, t in enumerate(sums)]
                for b in range(8):
                    D[s_, h, b, at, :] = sums[b].astype(BF16)
                return carry

            lax.fori_loop(0, 8, chunk, 0)

        for k in (2, 1, 3, 0):
            owner(m4(s + k))
            v = D.at[m4(s + k), h]
            if k == 2:
                net.send(f"R+{tag}", v.at[pl.ds(0, 4)], RL2.at[0, h], "s1")
                net.send(f"R-{tag}", v.at[pl.ds(4, 4)], RL2.at[1, h], "s3")
            elif k:
                net.send(f"D{k}{tag}", v, RD.at[s, h], f"s{k}")

    def forward_s(tag, h):
        net.wait(f"R+{tag}", RL2.at[0, 0])
        net.send(f"G+{tag}", RL2.at[0, h], RD.at[m4(s - 1), h, pl.ds(0, 4)], "s1")
        net.wait(f"R-{tag}", RL2.at[0, 0])
        net.send(f"G-{tag}", RL2.at[1, h], RD.at[m4(s + 1), h, pl.ds(4, 4)], "s3")

    def wait_s(tag):
        for k in (1, 3):
            net.wait(f"D{k}{tag}", RD.at[0, 0])
        net.wait(f"G+{tag}", RL2.at[0, 0])
        net.wait(f"G-{tag}", RL2.at[0, 0])

    def sum_s(h, b):
        total = D[s, h, b].astype(F32)
        for k in (1, 2, 3):
            total = total + RD[m4(s + k), h, b].astype(F32)
        return total

    forward_p("X", X)
    weight_1()
    for b in range(8):
        rows = jnp.zeros((128, 128), F32)
        for q in range(8):
            rows = rows + dot(QM[b, :, q * 128 : (q + 1) * 128], ACT[q])
        act_o[b * 128 : (b + 1) * 128, :] = rows.astype(BF16)
    wait_p("X")
    combine("X", X)
    weight_2()
    forward_p("x", x)
    forward_s("X", X)
    weight_3()
    wait_s("X")
    for b in range(8):
        FX[b] = sum_s(X, b).astype(BF16)
    net.send("fx", FX, FR, "x")
    wait_p("x")
    combine("x", x)
    weight_4()
    forward_s("x", x)
    weight_5()
    net.wait("fx", FR)
    wait_s("x")
    for b in range(8):
        GP[b] = (GA[b].astype(F32) + FR[b].astype(F32) + sum_s(x, b)).astype(BF16)
    for b in range(8):
        rows = jnp.zeros((128, 128), F32)
        for q in range(8):
            rows = rows + dot(QM[b, :, q * 128 : (q + 1) * 128], GP[q])
        gf_o[b * 128 : (b + 1) * 128, :] = rows.astype(BF16)
    for k in (1, 2, 3):
        net.wait(f"wq{k}", WF.at[0])
    for q in range(16):
        v = WF[q // 4, q % 4] * (65536.0**-0.5)
        u = jnp.concatenate([v[:, 128:], v[:, :128]], axis=1)
        gw_o[q * 8 : (q + 1) * 8, :] = jnp.where(f == 0, v, u)
    net.drain()


def local(features, weight, cotangent, tile_values, tile_owner, tile_block, tile_dest, node_order):
    pack = jnp.stack([tile_owner[:, 0], tile_block, tile_dest])
    pack = jnp.pad(pack, ((0, 5), (0, 32)), constant_values=200)
    vm, hbm = pl.BlockSpec(memory_space=pltpu.VMEM), pl.BlockSpec(memory_space=pl.ANY)
    V = pltpu.VMEM
    tile = (128, 128)
    return pl.pallas_call(
        kernel,
        name="graph_layer",
        out_shape=(
            jax.ShapeDtypeStruct((1024, 128), BF16),
            jax.ShapeDtypeStruct((1024, 128), BF16),
            jax.ShapeDtypeStruct((128, 256), F32),
        ),
        in_specs=[vm, vm, vm, vm, vm, hbm],
        out_specs=(vm, vm, vm),
        scratch_shapes=[
            V((512,) + tile, BF16), V((96,) + tile, BF16), V((128,) + tile, BF16), V((96,) + tile, F32),
            V((8, 128, 1024), BF16), V((8, 128, 1024), BF16), V((1024, 128), BF16), V((128, 256), BF16),
            V((128, 256), BF16), V((128, 256), BF16), V((8, 128, 256), BF16),
            V((8,) + tile, BF16), V((8,) + tile, BF16), V((8,) + tile, BF16), V((8,) + tile, BF16),
            V((4, 2, 4, 2) + tile, BF16), V((4, 2, 2, 4, 2) + tile, BF16), V((4, 2, 2, 4, 2) + tile, BF16),
            V((2, 2, 4, 2) + tile, BF16), V((4, 2, 8) + tile, BF16), V((4, 2, 8) + tile, BF16),
            V((2, 2, 4) + tile, BF16), V((8,) + tile, BF16), V((8,) + tile, BF16), V((8,) + tile, BF16),
            V((16, 128), I32), pltpu.SMEM((16, 128), I32), V((8, 8, 128), I32), pltpu.SMEM((8, 8, 128), I32),
            V((4, 32, 256), F32), V((4, 32, 256), F32), V((4, 8, 256), F32), V((4, 8, 256), F32),
            V((8, 256), F32), V((8, 256), F32), V((8, 256), F32), V((8, 256), F32), V((4, 4, 8, 256), F32),
            pltpu.SemaphoreType.DMA((NS,)), pltpu.SemaphoreType.DMA((NS,)), pltpu.SemaphoreType.DMA((2,)),
        ],
        compiler_params=pltpu.CompilerParams(collective_id=0, has_side_effects=True, vmem_limit_bytes=63 << 20),
    )(pack, node_order, features, weight, cotangent, tile_values)


def solution(mesh):
    return jax.shard_map(
        local,
        mesh=mesh,
        in_specs=(
            P("rows", "feat"), P("feat", None), P("rows", "feat"), P("rows", None, None),
            P("rows", None), P("rows"), P("rows"), P("rows", None),
        ),
        out_specs=(P("rows", "feat"), P("rows", "feat"), P("feat", None)),
        check_vma=False,
    )
```

```python
import jax
import jax.numpy as jnp
from jax import lax
from jax.experimental import pallas as pl
from jax.experimental.pallas import tpu as pltpu
from jax.sharding import PartitionSpec as P

MESH = pl.DeviceIdType.MESH
F32, BF16, I32 = jnp.float32, jnp.bfloat16, jnp.int32
NS = 190
F_TILE, F_SRC, F_DEST, F_CUM, B_TILE, B_DEST, B_BLK = range(7)


class Net:
    def __init__(self, ssem, rsem, targets):
        self.ssem, self.rsem, self.targets = ssem, rsem, targets
        self.names, self.sent = {}, []

    def copy(self, name, src, dst, to):
        i = self.names.setdefault(name, len(self.names))
        return pltpu.make_async_remote_copy(
            src, dst, self.ssem.at[i], self.rsem.at[i], device_id=self.targets[to], device_id_type=MESH
        )

    def send(self, name, src, dst, to):
        d = self.copy(name, src, dst, to)
        d.start()
        self.sent.append(d)

    def wait(self, name, view):
        self.copy(name, view, view, "c").wait_recv()

    def drain(self):
        for d in self.sent:
            d.wait_send()


def gather_blocks(G, net, x, y, z, c, fill):
    m4 = lambda v: lax.rem(v + 4, 4)
    X = 1 - x
    A = lambda z_, y_, x_: (((c * 4 + z_) * 4 + y_) * 2 + x_) * 3
    B = lambda y_, z_, x_: 192 + (((c * 4 + y_) * 4 + z_) * 2 + x_) * 3
    C1 = lambda x_, z_, y_: 384 + ((c * 2 + x_) * 4 + z_) * 4 + y_
    C2 = lambda x_, y_, z_: 448 + ((c * 2 + x_) * 4 + y_) * 4 + z_
    parts = []

    def view(idx, n, h=None):
        if h is None:
            return G.at[pl.ds(idx, n)]
        return G.at[idx, pl.ds(h * 64, 64)]

    def send(name, idx, n, to, h=None):
        v = view(idx, n, h)
        net.send(name, v, v, to)

    def fw(name, idx, n, h=None):
        send("p" + name, idx, n, "c", h)
        parts.append((name, n, h))

    def wait(name, n, h=None):
        net.wait(name, view(0, n, h))

    send('Cy+',C1(x,z,y),1,'y+'); send('Cy-',C1(x,z,y),1,'y-')
    send('Dz+',C2(x,y,z),1,'z+'); send('Dz-',C2(x,y,z),1,'z-')
    send('Ax',A(z,y,x),3,'x'); send('Bx',B(y,z,x),3,'x')
    send('Ay+o',A(z,y,x),3,'y+'); send('Ay-o',A(z,y,x),3,'y-')
    send('Bz+o',B(y,z,x),3,'z+'); send('Bz-o',B(y,z,x),3,'z-')
    fw('oA',A(z,y,x),3); fw('oB',B(y,z,x),3);
    yp,ym,y2=m4(y+1),m4(y-1),m4(y+2); zp,zm,z2=m4(z+1),m4(z-1),m4(z+2)
    wait('Ax',3); send('Ay+x',A(z,y,X),3,'y+'); send('Ay-x',A(z,y,X),3,'y-');
    wait('Bx',3); send('Bz+x',B(y,z,X),3,'z+'); send('Bz-x',B(y,z,X),3,'z-');
    wait('Cy+',1); send('Cy+f',C1(x,z,ym),1,'y+',0); wait('Cy-',1); send('Cy-f',C1(x,z,yp),1,'y-',1)
    wait('Dz+',1); send('Dz+f',C2(x,y,zm),1,'z+',0); wait('Dz-',1); send('Dz-f',C2(x,y,zp),1,'z-',1)
    send('Az+0',A(z,y,0),6,'z+'); send('Az-0',A(z,y,0),6,'z-')
    send('By+0',B(y,z,0),6,'y+'); send('By-0',B(y,z,0),6,'y-')
    fw('Ax',A(z,y,X),3); fw('Bx',B(y,z,X),3)
    wait('Ay+o',3); wait('Ay-o',3); wait('Ay+x',3); wait('Ay-x',3)
    send('Ay+f',A(z,ym,0),3,'y+'); send('Ay-f',A(z,yp,1),3,'y-')
    wait('Bz+o',3); wait('Bz-o',3); wait('Bz+x',3); wait('Bz-x',3)
    send('Bz+f',B(y,zm,0),3,'z+'); send('Bz-f',B(y,zp,1),3,'z-')
    wait('Cy+f',1,0); wait('Cy-f',1,1); send('Cz+',C1(x,z,0),4,'z+'); send('Cz-',C1(x,z,0),4,'z-')
    wait('Dz+f',1,0); wait('Dz-f',1,1); send('Dy+',C2(x,y,0),4,'y+'); send('Dy-',C2(x,y,0),4,'y-')
    send('Cx0',C1(x,z,0),4,'x'); send('Dx0',C2(x,y,0),4,'x')
    fw('C0',C1(x,z,0),4); fw('D0',C2(x,y,0),4)
    fill()
    for k,yy in ((1,ym),(3,yp)):
        send(f'Az+{k}',A(z,yy,0),6,'z+'); send(f'Az-{k}',A(z,yy,0),6,'z-')
        fw(f'Ay{k}',A(z,yy,0),6)
    for k,zz in ((1,zm),(3,zp)):
        send(f'By+{k}',B(y,zz,0),6,'y+'); send(f'By-{k}',B(y,zz,0),6,'y-')
        fw(f'Bz{k}',B(y,zz,0),6)
    fill()
    wait('Ay+f',3); wait('Ay-f',3)
    send('Az+2',A(z,y2,0),6,'z+'); send('Az-2',A(z,y2,0),6,'z-'); fw('Ay2',A(z,y2,0),6)
    wait('Bz+f',3); wait('Bz-f',3)
    send('By+2',B(y,z2,0),6,'y+'); send('By-2',B(y,z2,0),6,'y-'); fw('Bz2',B(y,z2,0),6)
    yk={0:y,1:ym,3:yp,2:y2}; zk={0:z,1:zm,3:zp,2:z2}
    def bulk(k):
        wait(f'Az+{k}',6); wait(f'Az-{k}',6)
        if k in (0,3): send(f'Az+f{k}',A(zm,yk[k],0),6,'z+')
        else: send(f'Az-f{k}',A(zp,yk[k],0),6,'z-')
        wait(f'By+{k}',6); wait(f'By-{k}',6)
        if k in (0,3): send(f'By+f{k}',B(ym,zk[k],0),6,'y+')
        else: send(f'By-f{k}',B(yp,zk[k],0),6,'y-')
        fw(f'Azm{k}',A(zm,yk[k],0),6); fw(f'Azp{k}',A(zp,yk[k],0),6)
        fw(f'Bym{k}',B(ym,zk[k],0),6); fw(f'Byp{k}',B(yp,zk[k],0),6)
    fill()
    bulk(0)
    fill()
    wait('Cz+',4); wait('Cz-',4); send('Cz+f',C1(x,zm,0),2,'z+'); send('Cz-f',C1(x,zp,2),2,'z-')
    wait('Dy+',4); wait('Dy-',4); send('Dy+f',C2(x,ym,0),2,'y+'); send('Dy-f',C2(x,yp,2),2,'y-')
    send('Cxm',C1(x,zm,0),4,'x'); send('Cxp',C1(x,zp,0),4,'x'); send('Dxm',C2(x,ym,0),4,'x'); send('Dxp',C2(x,yp,0),4,'x')
    fw('Czm',C1(x,zm,0),4); fw('Czp',C1(x,zp,0),4); fw('Dym',C2(x,ym,0),4); fw('Dyp',C2(x,yp,0),4)
    fill()
    bulk(1)
    fill()
    wait('Cz+f',2); wait('Cz-f',2); send('Cx2',C1(x,z2,0),4,'x'); fw('Cz2',C1(x,z2,0),4)
    wait('Dy+f',2); wait('Dy-f',2); send('Dx2',C2(x,y2,0),4,'x'); fw('Dy2',C2(x,y2,0),4)
    fill()
    bulk(3)
    fill()
    wait('Cx0',4); wait('Dx0',4); fw('Cx0',C1(X,z,0),4); fw('Dx0',C2(X,y,0),4)
    bulk(2)
    fill()
    for s,zz,yy in (('m',zm,ym),('p',zp,yp),('2',z2,y2)):
        wait('Cx'+s,4); fw('Cx'+s,C1(X,zz,0),4); wait('Dx'+s,4); fw('Dx'+s,C2(X,yy,0),4)
    for k in (0,1,3,2):
        d='+' if k in (0,3) else '-'
        wait(f'Az{d}f{k}',6); fw(f'Az2{k}',A(z2,yk[k],0),6)
        wait(f'By{d}f{k}',6); fw(f'By2{k}',B(y2,zk[k],0),6)
    fill()
    for name,n,h in parts: wait('p'+name,n,h)


def dot(a, b):
    return jnp.dot(a, b, preferred_element_type=F32)


def loop(n, body, unroll):
    def step(i, carry):
        body(i)
        return carry

    lax.fori_loop(0, n, step, 0, unroll=unroll)


def index_tables(pack, TAB):
    owner, block, dest = pack[0:1, :], pack[1:2, :], pack[2:3, :]
    sq = (128, 128)
    row = lambda v: jnp.broadcast_to(v, sq)
    col = lambda v: jnp.broadcast_to(v, sq).T
    i, j = lax.broadcasted_iota(I32, sq, 0), lax.broadcasted_iota(I32, sq, 1)
    count = lambda m: jnp.sum(jnp.where(m, 1, 0), axis=0, keepdims=True)
    co, cd, cb = col(owner), col(dest), col(block)
    rank = count((co == row(owner)) & (i < j))
    place = count((cd < row(dest)) | ((cd == row(dest)) & (i < j)))
    ox, oy, oz, oc = owner >> 5, (owner >> 3) & 3, (owner >> 1) & 3, owner & 1
    fa = (((oc * 4 + oz) * 4 + oy) * 2 + ox) * 3 + block
    fb = 192 + (((oc * 4 + oy) * 4 + oz) * 2 + ox) * 3 + block - 3
    fc = 384 + ((oc * 2 + ox) * 4 + oz) * 4 + oy
    fd = 448 + ((oc * 2 + ox) * 4 + oy) * 4 + oz
    src = jnp.where(block < 3, fa, jnp.where(block < 6, fb, jnp.where(block == 6, fc, fd)))
    op, os = jnp.where(oc == 0, oz, oy), jnp.where(oc == 0, oy, oz)
    slot = (((oc * 4 + op) * 2 + ox) * 4 + os) * 2 + rank
    live = lax.broadcasted_iota(I32, (1, 128), 1) < 96
    slot = jnp.where(live, slot, 999)
    cp, cs = col(place), col(slot)
    pick = lambda m, v: jnp.sum(jnp.where(m, v, 0), axis=0, keepdims=True)
    at_place, at_slot = cp == j, cs == j
    rows = [
        pick(at_place, i),
        pick(at_place, col(src)),
        pick(at_place, cd),
        count((cd <= j) & (i < 96)),
        pick(at_slot, i),
        pick(at_slot, cd),
        pick(at_slot, cb + 1) - 1,
    ]
    for r, (v, most) in enumerate(zip(rows, (95, 511, 7, 96, 95, 7, 7))):
        TAB[r : r + 1, :] = jnp.clip(v, -1 if r == B_BLK else 0, most)


def kernel(
    pack, order, feat, wt, cot, tiles, act_o, gf_o, gw_o,
    G, T, ST, SEG, PM, QM, CO, WO, WR, WOR, COT, AGG, AGO, GP, GA, OS, PP, RP, RL, D, RD, RL2, FX, FR, ACT,
    TAB, TABS, TV, NT, NTS, CP, RS, WG, WZ, W2, WS, W3, WX, W4, WC, WF, ssem, rsem, lsem,
):
    me, f = lax.axis_index("rows"), lax.axis_index("feat")
    x, y, z, c = me // 32, lax.rem(me // 8, 4), lax.rem(me // 2, 4), lax.rem(me, 2)
    p, s = (1 - c) * z + c * y, (1 - c) * y + c * z
    X, e = 1 - x, 1 - c
    m4 = lambda v: lax.rem(v + 4, 4)
    dev = lambda x_, y_, z_, c_: (((x_ * 4 + y_) * 4 + z_) * 2 + c_, f)
    dps = lambda p_, s_, c_: dev(x, (1 - c) * s_ + c * p_, (1 - c) * p_ + c * s_, c_)
    targets = {
        "x": dev(X, y, z, c), "y+": dev(x, m4(y + 1), z, c), "y-": dev(x, m4(y - 1), z, c),
        "z+": dev(x, y, m4(z + 1), c), "z-": dev(x, y, m4(z - 1), c), "c": dev(x, y, z, e), "f": (me, 1 - f),
    }
    for k in (1, 2, 3):
        targets[f"p{k}"], targets[f"s{k}"] = dps(m4(p + k), s, c), dps(p, m4(s + k), c)
        targets[f"P{k}"], targets[f"S{k}"] = dps(m4(p + k), s, e), dps(p, m4(s + k), e)
        targets[f"z{k}"], targets[f"y{k}"] = dev(x, y, m4(z + k), c), dev(x, m4(y + k), z, c)
    entry = lambda r, i, most: jnp.clip(TABS[r, i], 0, most)
    peers = ["x", "f", "c"] + [a + str(k) for a in "psPS" for k in (1, 2, 3)]
    bar = pltpu.get_barrier_semaphore()
    for n in peers:
        pl.semaphore_signal(bar, 1, device_id=targets[n], device_id_type=MESH)
    net = Net(ssem, rsem, targets)
    tile_copy = pltpu.make_async_copy(tiles, T, lsem.at[0])
    tile_copy.start()

    a0, b0 = (((c * 4 + z) * 4 + y) * 2 + x) * 3, 192 + (((c * 4 + y) * 4 + z) * 2 + x) * 3
    c0, d0 = 384 + ((c * 2 + x) * 4 + z) * 4 + y, 448 + ((c * 2 + x) * 4 + y) * 4 + z
    place = [a0, a0 + 1, a0 + 2, b0, b0 + 1, b0 + 2, c0, d0]
    lanes = lax.broadcasted_iota(I32, (128, 1024), 1).astype(F32)
    order_f = order[...].astype(F32)
    for b in range(8):
        oc = jnp.broadcast_to(order_f[:, b * 128 : (b + 1) * 128], (128, 128)).T
        hot = jnp.where(jnp.concatenate([oc] * 8, axis=1) == lanes, 1.0, 0.0).astype(BF16)
        PM[b] = hot
        G[place[b]] = dot(hot, feat[...]).astype(BF16)
    pl.semaphore_wait(bar, len(peers))

    def early():
        net.send("cot", cot, CO, "f")
        net.send("wt", wt, WO, "f")
        index_tables(pack, TAB)
        TV[p * 2 + c] = jnp.broadcast_to(TAB[B_BLK : B_BLK + 1, :], (8, 128))
        q = pltpu.make_async_copy(TAB, TABS, lsem.at[1])
        q.start()
        for k in (1, 2, 3):
            net.send(f"t{k}", TV.at[p * 2 + c], TV.at[p * 2 + c], f"p{k}")
        for k in (0, 1, 2, 3):
            net.send(f"u{k}", TV.at[p * 2 + c], TV.at[s * 2 + c], f"S{k}" if k else "c")
        q.wait()
        tile_copy.wait()

    def transposed(lo):
        def body(i):
            ST[lo + i] = T[entry(B_TILE, lo + i, 95)].T

        return lambda: loop(32, body, 8)

    def weights():
        net.wait("wt", WO)
        for src, dst in ((wt, WR), (WO, WOR)):
            v = src[...]
            u = jnp.concatenate([v[:, 128:], v[:, :128]], axis=1)
            dst[...] = jnp.where(f == 0, v, u)
        net.wait("cot", CO)

    def cotangents():
        def body(b):
            COT[b, :, 0:128] = dot(PM[b], cot[...]).astype(BF16)
            COT[b, :, 128:256] = dot(PM[b], CO[...]).astype(BF16)

        loop(8, body, 1)

    def inverse():
        def body(b):
            j = (lax.broadcasted_iota(I32, (128, 1024), 0) + b * 128).astype(F32)
            QM[b] = jnp.where(jnp.broadcast_to(order_f, (128, 1024)) == j, 1.0, 0.0).astype(BF16)

        loop(8, body, 1)

    def block_tables():
        for k in (1, 2, 3):
            net.wait(f"t{k}", TV.at[0])
        for k in (0, 1, 2, 3):
            net.wait(f"u{k}", TV.at[0])
        odd = lax.rem(lax.broadcasted_iota(I32, (8, 128), 1), 2)
        row = lax.broadcasted_iota(I32, (8, 128), 0)
        keys = []
        for n in range(8):
            k = jnp.where(TV[n] < 0, 8, TV[n]) * 16 + (2 * n + odd)
            keys += [k, jnp.where(odd == 0, pltpu.roll(k, 127, 1), pltpu.roll(k, 1, 1))]
        one = lambda m: jnp.where(m, 1, 0)
        low, high, ends = (jnp.zeros((8, 128), I32) for _ in range(3))
        for k in keys:
            at = sum(one(o < k) for o in keys)
            low, high = low + jnp.where(at == row, k, 0), high + jnp.where(at == row + 8, k, 0)
            ends = ends + one(k < (row + 1) * 16)
        NT[0:8, :], NT[8:16, :], NT[16:24, :] = low, high, ends
        q = pltpu.make_async_copy(NT, NTS, lsem.at[1])
        q.start()
        q.wait()

    fillers = [early, transposed(0), transposed(32), transposed(64), transposed(96), weights, cotangents, inverse, block_tables]

    def fill():
        if fillers:
            fillers.pop(0)()

    gather_blocks(G, net, x, y, z, c, fill)
    while fillers:
        fill()

    def product(i, total):
        fresh = (i == 0) | (TABS[F_DEST, i] != TABS[F_DEST, jnp.maximum(i - 1, 0)])
        total = total * jnp.where(fresh, 0.0, 1.0) + dot(T[entry(F_TILE, i, 95)], G[entry(F_SRC, i, 511)])
        SEG[i] = total
        return total

    lax.fori_loop(0, 96, product, jnp.zeros((128, 128), F32), unroll=8)
    for b in range(8):
        last = TABS[F_CUM, b]
        first = TABS[F_CUM, b - 1] if b else 0
        some = jnp.where(last > first, 1.0, 0.0)
        AGG[b] = (G[place[b]].astype(F32) + SEG[jnp.clip(last - 1, 0, 95)] * some).astype(BF16)
        net.send(f"agg{b}", AGG.at[b], AGO.at[b], "f")

    for b in range(8):
        net.wait(f"agg{b}", AGO.at[b])
        own = AGG[b]
        v = dot(own, WR[...]) + dot(AGO[b], WOR[...])
        t = jnp.tanh(0.7978845608 * (v + 0.044715 * (v * v * v)))
        half = 0.5 * (1.0 + t)
        ACT[b] = (v[:, :128] * half[:, :128]).astype(BF16)
        slope = half + 0.5 * v * (1.0 - t * t) * (0.7978845608 * (1.0 + 0.134145 * (v * v)))
        gp = (COT[b].astype(F32) * slope).astype(BF16)
        GA[b] = lax.dot_general(gp, WR[...], (((1,), (1,)), ((), ())), preferred_element_type=F32).astype(BF16)
        part = dot(own.T, gp)
        for q in range(4):
            rows = part[q * 32 : (q + 1) * 32]
            WG[q] = rows if b == 0 else WG[q] + rows

    for k in (1, 2, 3):
        net.send(f"wp{k}", WG.at[m4(z + k)], WZ.at[z], f"z{k}")

    def weight_1():
        for k in (1, 2, 3):
            net.wait(f"wp{k}", WZ.at[0])
        total = WG[z] + WZ[m4(z + 1)] + WZ[m4(z + 2)] + WZ[m4(z + 3)]
        for q in range(4):
            W2[q] = total[q * 8 : (q + 1) * 8]
        for k in (1, 2, 3):
            net.send(f"ws{k}", W2.at[m4(y + k)], WS.at[y], f"y{k}")

    def weight_2():
        for k in (1, 2, 3):
            net.wait(f"ws{k}", WS.at[0])
        W3[...] = W2[y] + WS[m4(y + 1)] + WS[m4(y + 2)] + WS[m4(y + 3)]
        net.send("wx", W3, WX, "x")

    def weight_3():
        net.wait("wx", WX)
        W4[...] = W3[...] + WX[...]
        net.send("wc", W4, WC, "c")

    def weight_4():
        net.wait("wc", WC)
        WF[z, y] = W4[...] + WC[...]
        for k in (1, 2, 3):
            net.send(f"wt{k}", WF.at[z, y], WF.at[z, y], f"y{k}")

    def weight_5():
        for k in (1, 2, 3):
            net.wait(f"wt{k}", WF.at[0, 0])
        for k in (1, 2, 3):
            net.send(f"wq{k}", WF.at[z], WF.at[z], f"z{k}")

    pp, ps = s, p

    def products(plane, p_, h, out):
        base = ((plane * 4 + p_) * 2 + h) * 8

        def body(i):
            out[i // 2, lax.rem(i, 2)] = dot(ST[base + i], GA[entry(B_DEST, base + i, 7)]).astype(BF16)

        loop(8, body, 8)

    def slab(h, k, own):
        q = m4(p + k)
        return (RP if k == 0 else PP).at[q, h]

    for tag, h in (("X", X), ("x", x)):
        for k in (2, 1, 3, 0):
            q, mine = m4(pp + k), m4(p + k)
            products(e, q, h, OS.at[q, h])
            net.send(f"i{tag}{k}", OS.at[q, h], (RP if k == 0 else PP).at[q, h, c], "c")
            products(c, mine, h, slab(h, k, True).at[c])
        for k in (2, 1, 3, 0):
            v = slab(h, k, True)
            net.wait(f"i{tag}{k}", v.at[0])
            if k == 2:
                net.send(f"r+{tag}", v.at[0], RL.at[0, h], "p1")
                net.send(f"r-{tag}", v.at[1], RL.at[1, h], "p3")
            elif k:
                net.send(f"d{k}{tag}", v, RP.at[p, h], f"p{k}")

    def forward_p(tag, h):
        net.wait(f"r+{tag}", RL.at[0, 0])
        net.send(f"g+{tag}", RL.at[0, h], RP.at[m4(p - 1), h, 0], "p1")
        net.wait(f"r-{tag}", RL.at[0, 0])
        net.send(f"g-{tag}", RL.at[1, h], RP.at[m4(p + 1), h, 1], "p3")

    def wait_p(tag):
        for k in (1, 3):
            net.wait(f"d{k}{tag}", RP.at[0, 0])
        net.wait(f"g+{tag}", RP.at[0, 0, 0])
        net.wait(f"g-{tag}", RP.at[0, 0, 0])

    def combine(tag, h):
        def owner(s_):
            q = (((c * 4 + p) * 2 + h) * 4 + s_) * 2
            for n in range(16):
                CP[n] = RP[n // 4, h, (n // 2) % 2, s_, n % 2]

            def step(j, total):
                k, before = NTS[j, q], NTS[jnp.maximum(j - 1, 0), q]
                fresh = (j == 0) | ((k >> 4) != (before >> 4))
                total = total * jnp.where(fresh, 0.0, 1.0) + CP[jnp.clip(k & 15, 0, 15)].astype(F32)
                RS[j] = total.astype(BF16)
                return total

            lax.fori_loop(0, 16, step, jnp.zeros((128, 128), F32), unroll=8)
            for b in range(8):
                last = NTS[16 + b, q]
                first = NTS[15 + b, q] if b else 0
                some = jnp.where(last > first, 1.0, 0.0)
                D[s_, h, b] = (RS[jnp.clip(last - 1, 0, 15)].astype(F32) * some).astype(BF16)

        for k in (2, 1, 3, 0):
            owner(m4(s + k))
            v = D.at[m4(s + k), h]
            if k == 2:
                net.send(f"R+{tag}", v.at[pl.ds(0, 4)], RL2.at[0, h], "s1")
                net.send(f"R-{tag}", v.at[pl.ds(4, 4)], RL2.at[1, h], "s3")
            elif k:
                net.send(f"D{k}{tag}", v, RD.at[s, h], f"s{k}")

    def forward_s(tag, h):
        net.wait(f"R+{tag}", RL2.at[0, 0])
        net.send(f"G+{tag}", RL2.at[0, h], RD.at[m4(s - 1), h, pl.ds(0, 4)], "s1")
        net.wait(f"R-{tag}", RL2.at[0, 0])
        net.send(f"G-{tag}", RL2.at[1, h], RD.at[m4(s + 1), h, pl.ds(4, 4)], "s3")

    def wait_s(tag):
        for k in (1, 3):
            net.wait(f"D{k}{tag}", RD.at[0, 0])
        net.wait(f"G+{tag}", RL2.at[0, 0])
        net.wait(f"G-{tag}", RL2.at[0, 0])

    def sum_s(h, b):
        total = D[s, h, b].astype(F32)
        for k in (1, 2, 3):
            total = total + RD[m4(s + k), h, b].astype(F32)
        return total

    forward_p("X", X)
    weight_1()
    for b in range(8):
        rows = jnp.zeros((128, 128), F32)
        for q in range(8):
            rows = rows + dot(QM[b, :, q * 128 : (q + 1) * 128], ACT[q])
        act_o[b * 128 : (b + 1) * 128, :] = rows.astype(BF16)
    wait_p("X")
    combine("X", X)
    weight_2()
    forward_p("x", x)
    forward_s("X", X)
    weight_3()
    wait_s("X")
    for b in range(8):
        FX[b] = sum_s(X, b).astype(BF16)
    net.send("fx", FX, FR, "x")
    wait_p("x")
    combine("x", x)
    weight_4()
    forward_s("x", x)
    weight_5()
    net.wait("fx", FR)
    wait_s("x")
    for b in range(8):
        GP[b] = (GA[b].astype(F32) + FR[b].astype(F32) + sum_s(x, b)).astype(BF16)
    for b in range(8):
        rows = jnp.zeros((128, 128), F32)
        for q in range(8):
            rows = rows + dot(QM[b, :, q * 128 : (q + 1) * 128], GP[q])
        gf_o[b * 128 : (b + 1) * 128, :] = rows.astype(BF16)
    for k in (1, 2, 3):
        net.wait(f"wq{k}", WF.at[0])
    for q in range(16):
        v = WF[q // 4, q % 4] * (65536.0**-0.5)
        u = jnp.concatenate([v[:, 128:], v[:, :128]], axis=1)
        gw_o[q * 8 : (q + 1) * 8, :] = jnp.where(f == 0, v, u)
    net.drain()


def local(features, weight, cotangent, tile_values, tile_owner, tile_block, tile_dest, node_order):
    pack = jnp.stack([tile_owner[:, 0], tile_block, tile_dest])
    pack = jnp.pad(pack, ((0, 5), (0, 32)), constant_values=200)
    vm, hbm = pl.BlockSpec(memory_space=pltpu.VMEM), pl.BlockSpec(memory_space=pl.ANY)
    V = pltpu.VMEM
    tile = (128, 128)
    return pl.pallas_call(
        kernel,
        name="graph_layer",
        out_shape=(
            jax.ShapeDtypeStruct((1024, 128), BF16),
            jax.ShapeDtypeStruct((1024, 128), BF16),
            jax.ShapeDtypeStruct((128, 256), F32),
        ),
        in_specs=[vm, vm, vm, vm, vm, hbm],
        out_specs=(vm, vm, vm),
        scratch_shapes=[
            V((512,) + tile, BF16), V((96,) + tile, BF16), V((128,) + tile, BF16), V((96,) + tile, F32),
            V((8, 128, 1024), BF16), V((8, 128, 1024), BF16), V((1024, 128), BF16), V((128, 256), BF16),
            V((128, 256), BF16), V((128, 256), BF16), V((8, 128, 256), BF16),
            V((8,) + tile, BF16), V((8,) + tile, BF16), V((8,) + tile, BF16), V((8,) + tile, BF16),
            V((4, 2, 4, 2) + tile, BF16), V((4, 2, 2, 4, 2) + tile, BF16), V((4, 2, 2, 4, 2) + tile, BF16),
            V((2, 2, 4, 2) + tile, BF16), V((4, 2, 8) + tile, BF16), V((4, 2, 8) + tile, BF16),
            V((2, 2, 4) + tile, BF16), V((8,) + tile, BF16), V((8,) + tile, BF16), V((8,) + tile, BF16),
            V((16, 128), I32), pltpu.SMEM((16, 128), I32), V((8, 8, 128), I32),
            V((24, 128), I32), pltpu.SMEM((24, 128), I32), V((16,) + tile, BF16), V((16,) + tile, BF16),
            V((4, 32, 256), F32), V((4, 32, 256), F32), V((4, 8, 256), F32), V((4, 8, 256), F32),
            V((8, 256), F32), V((8, 256), F32), V((8, 256), F32), V((8, 256), F32), V((4, 4, 8, 256), F32),
            pltpu.SemaphoreType.DMA((NS,)), pltpu.SemaphoreType.DMA((NS,)), pltpu.SemaphoreType.DMA((2,)),
        ],
        compiler_params=pltpu.CompilerParams(collective_id=0, has_side_effects=True, vmem_limit_bytes=63 << 20),
    )(pack, node_order, features, weight, cotangent, tile_values)


def solution(mesh):
    return jax.shard_map(
        local,
        mesh=mesh,
        in_specs=(
            P("rows", "feat"), P("feat", None), P("rows", "feat"), P("rows", None, None),
            P("rows", None), P("rows"), P("rows"), P("rows", None),
        ),
        out_specs=(P("rows", "feat"), P("rows", "feat"), P("feat", None)),
        check_vma=False,
    )
```
